32 devices in a mesh: grp: 2 (over x), col: 16 (over z, y, core).
Axes of the slice: x: 2, y: 2, z: 4, core: 2. Of those that a mesh axis runs over, the one named last changes fastest.
Arguments:
- leaf_right_hand: float32 [320, 256, 128], P(('grp', 'col')), parts along dimension 0, may hold values from -6 to 6
- leaf_diagonal_inverse: bfloat16 [320, 256, 256], P(('grp', 'col')), parts along dimension 0, as said below
- leaf_coupling: bfloat16 [320, 4, 256, 256], P(('grp', 'col')), parts along dimension 0, may hold values from -0.03125 to 0.03125
- leaf_pattern: int32 [320, 4], P(('grp', 'col')), parts along dimension 0, may hold values 0 or 1
- top_rhs: float32 [32, 256, 128], P(('grp', 'col')), parts along dimension 0, may hold values from -6 to 6
- top_inverse: bfloat16 [32, 256, 256], P(('grp', 'col')), parts along dimension 0, as said below
- top_coupling: bfloat16 [32, 4, 256, 256], P(('grp', 'col')), parts along dimension 0, may hold values from -0.09375 to 0.09375
Outputs:
- leaf_solution: float32 [320, 256, 128], P(('grp', 'col')), parts along dimension 0
- top_solution: float32 [32, 256, 128], P(('grp', 'col')), parts along dimension 0
The draws below stay inside these ranges and needn't reach their ends.
There are 2 independent parts, one for each index of `grp`. The reference program is written for one: setup_inputs(seed, part) draws one part's arguments, and reference() takes and returns one part's arrays. A program takes and returns all parts, laid end to end along the dimension named above; each array names one. Nothing has to cross between parts.
Inputs may be any that keep to these rules, and one draw needn't show every extreme that they name: `leaf_diagonal_inverse`: lower triangular, diagonal between 0.7 and 1.3. `top_inverse`: lower triangular, diagonal between 0.7 and 1.3.
All inputs are finite; a program needn't handle non-finite values. No bound on the sum of `leaf_pattern` on one device may be relied on, other than what follows from the above.
Results may differ from the reference program's by a relative error of at most 0.0044.
Values sent between devices are 32-bit elements; how exact they have to be, the bound alone decides.
No kernel may reach another device: no remote copies, remote signals or barrier semaphores. Data moves between devices by JAX's collectives and lax.ppermute only.
A program may use at most 64 MiB of HBM per device.

```python
import math
import jax
import jax.numpy as jnp
import numpy as np
from jax import lax

SN_WIDTH = 256
RHS = 128
LEAVES = 10
LEVELS = 4
N_COL = 16


def triangle(diag_key, lower, blocks, width):
    rows = lax.broadcasted_iota(jnp.int32, (width, width), 0)
    cols = lax.broadcasted_iota(jnp.int32, (width, width), 1)
    diagonal = jax.random.uniform(diag_key, (blocks, width, 1), jnp.float32, 0.7, 1.3)
    result = jnp.where(rows > cols, lower, 0.0) + jnp.where(rows == cols, diagonal, 0.0)
    return result.astype(jnp.bfloat16)


def draw_leaf_diagonal_inverse(key, part):
    diag_key = jax.random.fold_in(key, 11)
    low_key = jax.random.fold_in(key, 12)
    shape = (N_COL * LEAVES, SN_WIDTH, SN_WIDTH)
    lower = jax.random.truncated_normal(low_key, -4.0, 4.0, shape, jnp.float32) * (0.6 / math.sqrt(SN_WIDTH))
    return triangle(diag_key, lower, N_COL * LEAVES, SN_WIDTH)


def draw_top_inverse(key, part):
    diag_key = jax.random.fold_in(key, 21)
    low_key = jax.random.fold_in(key, 22)
    shape = (N_COL, SN_WIDTH, SN_WIDTH)
    lower = jax.random.truncated_normal(low_key, -4.0, 4.0, shape, jnp.float32) * (0.6 / math.sqrt(SN_WIDTH))
    return triangle(diag_key, lower, N_COL, SN_WIDTH)


def with_ends(array, rng, least, top_value):
    shape = array.shape
    place = [jax.random.randint(jax.random.fold_in(rng, axis), (), 0, shape[axis]) for axis in range(len(shape))]
    array = array.at[tuple(place)].set(least)
    longest = shape.index(max(shape))
    place[longest] = (place[longest] + 1) % shape[longest]
    return array.at[tuple(place)].set(top_value)


def steps_of(rng, extent, split, low, high):
    gain, own = 1.0, jax.random.fold_in(rng, 6)
    for dim, shards_of in split:
        steps = jnp.exp(jax.random.uniform(jax.random.fold_in(own, dim), (shards_of,), jnp.float32, low / len(split), high / len(split)))
        gain = gain * jnp.repeat(steps, extent[dim] // shards_of).reshape([-1 if axis == dim else 1 for axis in range(len(extent))])
    return gain


def gaussian(key, extent, scale, reach, split=(), kind=jnp.bfloat16):
    array = jax.random.normal(key, extent, jnp.float32) * scale
    if len(split) > 0:
        array = steps_of(key, extent, split, -0.22, 0.18) * array
    return jnp.clip(array, min=-reach, max=reach).astype(kind)


def setup_inputs(seed: int = 0, part: int = 0) -> dict:
    keys = jax.random.split(jax.random.key(seed), 8)
    own_keys = jax.random.split(jax.random.fold_in(keys[7], part), 8)
    leaf_right_hand = gaussian(own_keys[0], (N_COL * LEAVES, SN_WIDTH, RHS), 1.0, 6.0, ((0, 16),), jnp.float32)
    leaf_diagonal_inverse = draw_leaf_diagonal_inverse(jax.random.fold_in(jax.random.fold_in(keys[7], part), 71), part)
    leaf_coupling = gaussian(own_keys[2], (N_COL * LEAVES, LEVELS, SN_WIDTH, SN_WIDTH), (SN_WIDTH * LEAVES * N_COL) ** -0.5, 0.03125, ((0, 16),))
    leaf_pattern = with_ends((jax.random.randint(own_keys[3], (N_COL * LEAVES, LEVELS), 0, 4) < 3).astype(jnp.int32), jax.random.fold_in(own_keys[3], 1), 0, 1)
    top_rhs = gaussian(own_keys[4], (N_COL, SN_WIDTH, RHS), 1.0, 6.0, ((0, 16),), jnp.float32)
    top_inverse = draw_top_inverse(jax.random.fold_in(jax.random.fold_in(keys[7], part), 71), part)
    top_coupling = gaussian(own_keys[6], (N_COL, LEVELS, SN_WIDTH, SN_WIDTH), (SN_WIDTH * N_COL) ** -0.5, 0.09375, ((0, 16),))
    return {"leaf_right_hand": leaf_right_hand, "leaf_diagonal_inverse": leaf_diagonal_inverse, "leaf_coupling": leaf_coupling, "leaf_pattern": leaf_pattern, "top_rhs": top_rhs, "top_inverse": top_inverse, "top_coupling": top_coupling}


def random_key(value):
    return lax.optimization_barrier(value.astype(jnp.bfloat16)).astype(jnp.float32)


def leaf_up(inputs):
    right_hand_block, block_inverse, coupling_block, pattern_block = inputs
    forward_sweep = jnp.einsum("efj,ejs->efs", block_inverse.astype(jnp.float32), random_key(right_hand_block))
    masked = pattern_block.astype(jnp.float32)[:, :, None, None] * random_key(forward_sweep)[:, None]
    terms = jnp.einsum("ikab,ikbr->kar", coupling_block.astype(jnp.float32), masked)
    return forward_sweep, terms


def leaf_down(inputs):
    forward_sweep, block_inverse, coupling_block, pattern_block, path_block = inputs
    masked = pattern_block.astype(jnp.float32)[:, :, None, None] * random_key(path_block)[None]
    carried_value = jnp.einsum("ikab,ikar->ibr", coupling_block.astype(jnp.float32), masked)
    return jnp.einsum("vdu,vdo->vuo", block_inverse.astype(jnp.float32), random_key(forward_sweep - carried_value))


def reference(leaf_right_hand, leaf_diagonal_inverse, leaf_coupling, leaf_pattern, top_rhs, top_inverse, top_coupling):
    count = N_COL
    depth = LEVELS
    shaped_rhs = leaf_right_hand.reshape(count, LEAVES, SN_WIDTH, RHS)
    shaped_inverse = leaf_diagonal_inverse.reshape(count, LEAVES, SN_WIDTH, SN_WIDTH)
    shaped_coupling = leaf_coupling.reshape(count, LEAVES, depth, SN_WIDTH, SN_WIDTH)
    shaped_pattern = leaf_pattern.reshape(count, LEAVES, depth)
    leaf_forward, leaf_terms = lax.map(leaf_up, (shaped_rhs, shaped_inverse, shaped_coupling, shaped_pattern))
    top_terms = jnp.zeros((count, depth, SN_WIDTH, RHS), jnp.float32)
    top_forward = jnp.zeros((count, SN_WIDTH, RHS), jnp.float32)
    for level in reversed(range(depth)):
        group = 2 ** (depth - level)
        owners = np.arange(2 ** level) * group + group // 2 - 1
        gathered = (leaf_terms[:, level] + top_terms[:, level]).reshape(2 ** level, group, SN_WIDTH, RHS).sum(axis=1)
        solved = jnp.einsum("nab,nbr->nar", top_inverse[owners].astype(jnp.float32), random_key(top_rhs[owners] - gathered))
        top_forward = top_forward.at[owners].set(solved)
        if level > 0:
            upward = jnp.einsum("nkab,nbr->nkar", top_coupling[owners, :level].astype(jnp.float32), random_key(solved))
            top_terms = top_terms.at[owners, :level].set(upward)
    path_values = jnp.zeros((count, depth, SN_WIDTH, RHS), jnp.float32)
    top_solution = jnp.zeros((count, SN_WIDTH, RHS), jnp.float32)
    for level in range(depth):
        group = 2 ** (depth - level)
        owners = np.arange(2 ** level) * group + group // 2 - 1
        base = top_forward[owners]
        if level > 0:
            known = path_values[owners, :level]
            carried_value = jnp.einsum("nkab,nkar->nbr", top_coupling[owners, :level].astype(jnp.float32), random_key(known))
            base = base - carried_value
        solved = jnp.einsum("nab,nar->nbr", top_inverse[owners].astype(jnp.float32), random_key(base))
        top_solution = top_solution.at[owners].set(solved)
        path_values = path_values.at[:, level].set(jnp.repeat(solved, group, axis=0))
    top_solution = top_solution.at[count - 1].set(path_values[count - 1, 0])
    leaf_solution = lax.map(leaf_down, (leaf_forward, shaped_inverse, shaped_coupling, shaped_pattern, path_values))
    return leaf_solution.reshape(count * LEAVES, SN_WIDTH, RHS), top_solution
```

```python
import jax
import jax.numpy as jnp
from jax import lax
from jax.experimental import pallas as pl
from jax.experimental.pallas import tpu as pltpu
from jax.sharding import PartitionSpec as P

SMEM = pl.BlockSpec(memory_space=pltpu.SMEM)
VMEM = pl.BlockSpec(memory_space=pltpu.VMEM)
F32 = jnp.float32
BF16 = jnp.bfloat16


def swap(value, mask):
    count = lax.axis_size("col")
    return lax.ppermute(value, "col", [(i, i ^ mask) for i in range(count)])


def times(a, b):
    return lax.dot_general(a, b, (((1,), (0,)), ((), ())), preferred_element_type=F32)


def times_transposed(a, b):
    return lax.dot_general(a, b, (((1,), (1,)), ((), ())), preferred_element_type=F32)


def call(kernel, out_shape, in_specs, flops, bytes_accessed, name, **kwargs):
    return pl.pallas_call(
        kernel,
        out_shape=out_shape,
        in_specs=in_specs,
        name=name,
        cost_estimate=pl.CostEstimate(
            flops=flops, bytes_accessed=bytes_accessed, transcendentals=0
        ),
        **kwargs,
    )


def leaf_up(meta, pattern, right_hand, inverse, coupling, top_rhs):
    leaves, width, columns = right_hand.shape
    depth = coupling.shape[1]
    half = columns // 2

    def kernel(meta_ref, pat_ref, rhs_ref, inv_ref, cpl_ref, top_ref, fwd_ref, keep_ref, send_ref, acc):
        leaf = pl.program_id(0)
        solved = times(inv_ref[0], rhs_ref[0].astype(BF16))
        fwd_ref[0] = solved.T
        rounded = solved.astype(BF16)
        for k in range(depth):
            present = (pat_ref[leaf, k] != 0).astype(F32)
            term = present * times(cpl_ref[0, k], rounded)

            @pl.when(leaf == 0)
            def _():
                acc[k] = term

            @pl.when(leaf > 0)
            def _():
                acc[k] = acc[k] + term

        @pl.when(leaf == leaves - 1)
        def _():
            core = meta_ref[0]
            for k in range(depth):
                mine = (meta_ref[1] == k).astype(F32)
                acc[k] = acc[k] - mine * top_ref[0]
                flipped = acc[k].T

                @pl.when(core == 0)
                def _():
                    keep_ref[k] = flipped[:half]
                    send_ref[k] = flipped[half:]

                @pl.when(core != 0)
                def _():
                    keep_ref[k] = flipped[half:]
                    send_ref[k] = flipped[:half]

    part = jax.ShapeDtypeStruct((depth, half, width), F32)
    whole = pl.BlockSpec((depth, half, width), lambda i: (0, 0, 0))
    return call(
        kernel,
        (jax.ShapeDtypeStruct((leaves, columns, width), F32), part, part),
        [
            SMEM,
            SMEM,
            pl.BlockSpec((1, width, columns), lambda i: (i, 0, 0)),
            pl.BlockSpec((1, width, width), lambda i: (i, 0, 0)),
            pl.BlockSpec((1, depth, width, width), lambda i: (i, 0, 0, 0)),
            pl.BlockSpec((1, width, columns), lambda i: (0, 0, 0)),
        ],
        2 * leaves * (depth + 1) * width * width * columns,
        leaves * width * (width * 2 * (depth + 1) + columns * 8),
        "leaf_up",
        grid=(leaves,),
        out_specs=(pl.BlockSpec((1, columns, width), lambda i: (i, 0, 0)), whole, whole),
        scratch_shapes=[pltpu.VMEM((depth, width, columns), F32)],
    )(meta, pattern, right_hand, inverse, coupling, top_rhs)


def node_up(mine, theirs, factors, level, name):
    half, width = mine.shape

    def kernel(mine_ref, theirs_ref, w_ref, fwd_ref, *up_ref):
        total = mine_ref[...] + theirs_ref[...]
        solved = times_transposed((-total).astype(BF16), w_ref[0].astype(BF16))
        fwd_ref[...] = solved
        rounded = solved.astype(BF16)
        for k in range(level):
            up_ref[0][k] = times_transposed(rounded, w_ref[1 + k].astype(BF16))

    shapes = [jax.ShapeDtypeStruct((half, width), F32)]
    if level > 0:
        shapes.append(jax.ShapeDtypeStruct((level, half, width), F32))
    return call(
        kernel,
        tuple(shapes),
        [VMEM] * 3,
        2 * (1 + level) * half * width * width,
        4 * (1 + level) * width * width,
        name,
        out_specs=(VMEM,) * len(shapes),
    )(mine, theirs, factors)


def top_down(mine, theirs, forwards, factors):
    half, width = mine.shape
    levels = len(factors)
    n = len(forwards)

    def kernel(mine_ref, theirs_ref, *refs):
        fwd, w, out = refs[:n], refs[n : n + levels], refs[n + levels]
        total = mine_ref[...] + theirs_ref[...]
        inverse = w[0][0].astype(BF16)
        base = times_transposed((-total).astype(BF16), inverse)
        rounded = []
        for level in range(levels):
            if level > 0:
                base = fwd[level - 1][...]
                carried = times(rounded[0], w[level][1].astype(BF16))
                for k in range(1, level):
                    carried = carried + times(rounded[k], w[level][1 + k].astype(BF16))
                base = base - carried
            solved = times(base.astype(BF16), w[level][0].astype(BF16))
            out[level] = solved
            rounded.append(solved.astype(BF16))

    return call(
        kernel,
        jax.ShapeDtypeStruct((levels, half, width), F32),
        [VMEM] * (2 + n + levels),
        2 * (levels + 1) * half * width * width,
        4 * levels * width * width,
        "top_down",
        out_specs=VMEM,
    )(mine, theirs, *forwards, *factors)


def node_down(use_theirs, mine, theirs, forward, factors, name):
    level, half, width = mine.shape

    def kernel(flag_ref, mine_ref, theirs_ref, fwd_ref, w_ref, out_ref):
        take = flag_ref[0] != 0
        carried = None
        for k in range(level):
            known = jnp.where(take, theirs_ref[k], mine_ref[k])
            out_ref[k] = known
            term = times(known.astype(BF16), w_ref[1 + k].astype(BF16))
            carried = term if carried is None else carried + term
        base = (fwd_ref[...] - carried).astype(BF16)
        out_ref[level] = times(base, w_ref[0].astype(BF16))

    return call(
        kernel,
        jax.ShapeDtypeStruct((level + 1, half, width), F32),
        [SMEM] + [VMEM] * 4,
        2 * (1 + level) * half * width * width,
        4 * (1 + level) * width * width,
        name,
        out_specs=VMEM,
    )(use_theirs, mine, theirs, forward, factors)


def leaf_down(meta, pattern, mine, theirs, forward, inverse, coupling):
    leaves, columns, width = forward.shape
    depth = coupling.shape[1]
    half = columns // 2

    def kernel(meta_ref, pat_ref, mine_ref, theirs_ref, fwd_ref, inv_ref, cpl_ref, out_ref, top_ref, path):
        leaf = pl.program_id(0)

        @pl.when(leaf == 0)
        def _():
            core = meta_ref[0]
            own = jnp.maximum(meta_ref[1], 0)

            @pl.when(core == 0)
            def _():
                for k in range(depth):
                    path[k, :half] = mine_ref[k].astype(BF16)
                    path[k, half:] = theirs_ref[k].astype(BF16)
                top_ref[0, :, :] = jnp.concatenate([mine_ref[own], theirs_ref[own]], axis=0).T

            @pl.when(core != 0)
            def _():
                for k in range(depth):
                    path[k, :half] = theirs_ref[k].astype(BF16)
                    path[k, half:] = mine_ref[k].astype(BF16)
                top_ref[0, :, :] = jnp.concatenate([theirs_ref[own], mine_ref[own]], axis=0).T

        carried = jnp.zeros((columns, width), F32)
        for k in range(depth):
            present = (pat_ref[leaf, k] != 0).astype(F32)
            carried = carried + present * times(path[k], cpl_ref[0, k])
        base = (fwd_ref[0] - carried).astype(BF16)
        out_ref[0] = times(base, inv_ref[0]).T

    fixed = pl.BlockSpec((depth, half, width), lambda i: (0, 0, 0))
    return call(
        kernel,
        (
            jax.ShapeDtypeStruct((leaves, width, columns), F32),
            jax.ShapeDtypeStruct((1, width, columns), F32),
        ),
        [
            SMEM,
            SMEM,
            fixed,
            fixed,
            pl.BlockSpec((1, columns, width), lambda i: (i, 0, 0)),
            pl.BlockSpec((1, width, width), lambda i: (i, 0, 0)),
            pl.BlockSpec((1, depth, width, width), lambda i: (i, 0, 0, 0)),
        ],
        2 * leaves * (depth + 1) * width * width * columns,
        leaves * width * (width * 2 * (depth + 1) + columns * 8),
        "leaf_down",
        grid=(leaves,),
        out_specs=(
            pl.BlockSpec((1, width, columns), lambda i: (i, 0, 0)),
            pl.BlockSpec((1, width, columns), lambda i: (0, 0, 0)),
        ),
        scratch_shapes=[pltpu.VMEM((depth, columns, width), BF16)],
    )(meta, pattern, mine, theirs, forward, inverse, coupling)


def local(
    leaf_right_hand,
    leaf_diagonal_inverse,
    leaf_coupling,
    leaf_pattern,
    top_rhs,
    top_inverse,
    top_coupling,
):
    depth = lax.axis_size("col").bit_length() - 1
    device = lax.axis_index("col")
    width = top_inverse.shape[1]
    rows = width // 2

    def bit(b):
        return device >> b & 1

    core = bit(0)
    run, trailing = 1, 0
    for b in range(depth):
        run = run * bit(b)
        trailing = trailing + run
    own_level = depth - 1 - trailing
    meta = jnp.where(jnp.arange(2) == 0, core, own_level).astype(jnp.int32)

    own_factors = jnp.concatenate([top_inverse, top_coupling[0, : depth - 1]]).astype(F32)
    other_factors = swap(own_factors, 1)
    factors = [None] * depth
    factors[depth - 1] = jnp.where(core == 0, own_factors, other_factors)
    upper = jnp.where(core == 0, other_factors, own_factors)[: depth - 1]
    factors[depth - 2] = upper

    forward, keep, send = leaf_up(
        meta, leaf_pattern, leaf_right_hand, leaf_diagonal_inverse, leaf_coupling, top_rhs
    )

    def both_halves(part):
        other = swap(part, 1)
        first = jnp.where(core == 0, part, other)
        second = jnp.where(core == 0, other, part)
        return jnp.concatenate([first, second], axis=1)

    hub = swap(lax.dynamic_slice_in_dim(upper[: depth - 2], core * rows, rows, 1), 2)
    factors[depth - 3] = both_halves(hub)
    spread = [swap(hub[: depth - 3], 4 | m << 3) for m in range(1 << (depth - 3))]
    for b in range(3, depth):
        level = depth - 1 - b
        index = bit(b) << (b - 3)
        for i in range(3, b):
            index = index | (1 - bit(i)) << (i - 3)
        part = spread[0][: level + 1]
        for m in range(1, 1 << (b - 2)):
            part = jnp.where(index == m, spread[m][: level + 1], part)
        factors[level] = both_halves(part)

    theirs = swap(send, 1)
    forwards = [None] * depth
    rest = keep + theirs
    mine, other = keep[depth - 1], theirs[depth - 1]
    for level in reversed(range(1, depth)):
        solved, terms = node_up(mine, other, factors[level], level, f"node_up_{level}")
        forwards[level] = solved
        rest = rest[:level] + terms
        mine = rest[level - 1]
        other = swap(mine, 1 << (depth - level))
        if level > 1:
            rest = rest[: level - 1] + swap(rest[: level - 1], 1 << (depth - level))

    known = top_down(mine, other, forwards[1 : depth - 2], factors[: depth - 2])
    for level in (depth - 2, depth - 1):
        b = depth - level
        use_theirs = jnp.full((1,), bit(b), jnp.int32)
        known = node_down(
            use_theirs,
            known,
            swap(known, 1 << b),
            forwards[level],
            factors[level],
            f"node_down_{level}",
        )
    return leaf_down(
        meta,
        leaf_pattern,
        known,
        swap(known, 1),
        forward,
        leaf_diagonal_inverse,
        leaf_coupling,
    )


def solution(mesh):
    in_specs = (
        P(("grp", "col"), None, None),
        P(("grp", "col"), None, None),
        P(("grp", "col"), None, None, None),
        P(("grp", "col"), None),
        P(("grp", "col"), None, None),
        P(("grp", "col"), None, None),
        P(("grp", "col"), None, None, None),
    )
    out_specs = (P(("grp", "col"), None, None), P(("grp", "col"), None, None))
    return jax.shard_map(local, mesh=mesh, in_specs=in_specs, out_specs=out_specs, check_vma=False)
```

```python
import jax
import jax.numpy as jnp
from jax import lax
from jax.experimental import pallas as pl
from jax.experimental.pallas import tpu as pltpu
from jax.sharding import PartitionSpec as P

F32 = jnp.float32
BF16 = jnp.bfloat16
ANY = pl.BlockSpec(memory_space=pl.ANY)
VMEM = pl.BlockSpec(memory_space=pltpu.VMEM)


def swap(value, mask):
    count = lax.axis_size("col")
    return lax.ppermute(value, "col", [(i, i ^ mask) for i in range(count)])


def dot(a, b, dim_a, dim_b):
    return lax.dot_general(a, b, (((dim_a,), (dim_b,)), ((), ())), preferred_element_type=F32)


def bit_of(b):
    return lax.axis_index("col") >> b & 1


def level_of_own_node():
    depth = lax.axis_size("col").bit_length() - 1
    run, trailing = 1, 0
    for b in range(depth):
        run = run * bit_of(b)
        trailing = trailing + run
    return depth - 1 - trailing


def call(kernel, name, outs, ins, flops=0, hbm_ins=(), hbm_outs=(), scratch=(), limit=4 << 20):
    pinned = [pltpu.with_memory_space_constraint(x, pltpu.VMEM) for x in ins]
    shapes = [jax.ShapeDtypeStruct(s, d) for s, d in hbm_outs] + [pltpu.VMEM(s, d) for s, d in outs]
    moved = sum(x.size * x.dtype.itemsize for x in hbm_ins)
    result = pl.pallas_call(
        kernel,
        out_shape=tuple(shapes),
        in_specs=[ANY] * len(hbm_ins) + [VMEM] * len(ins),
        out_specs=tuple([ANY] * len(hbm_outs) + [VMEM] * len(outs)),
        scratch_shapes=list(scratch),
        name=name,
        compiler_params=pltpu.CompilerParams(vmem_limit_bytes=limit),
        cost_estimate=pl.CostEstimate(flops=flops, bytes_accessed=moved + 1024, transcendentals=0),
    )(*hbm_ins, *pinned)
    return result


def split_columns(terms, keep_ref, send_ref, place):
    half = terms.shape[0] // 2

    @pl.when(bit_of(0) == 0)
    def _():
        keep_ref[place] = terms[:half]
        send_ref[place] = terms[half:]

    @pl.when(bit_of(0) != 0)
    def _():
        keep_ref[place] = terms[half:]
        send_ref[place] = terms[:half]


def leaf_terms(first, pattern, coupling, levels, top_rhs, right_hand=None, inverse=None, rounded=None):
    leaves, _, width, _ = coupling.shape
    columns = top_rhs.shape[2]
    half = columns // 2
    n = len(levels)
    start = levels[0]

    def kernel(pat_hbm, cpl_hbm, top_ref, *refs):
        if first:
            rhs_ref, inv_ref, keep_ref, send_ref, cpl_ref, fwd_ref, rnd_ref, pat_ref, pat_sem, sem = refs
        else:
            rnd_ref, keep_ref, send_ref, cpl_ref, pat_ref, pat_sem, sem = refs
        get_pattern = pltpu.make_async_copy(pat_hbm, pat_ref, pat_sem)
        get_pattern.start()
        fetches = []
        for i in range(leaves):
            fetch = pltpu.make_async_copy(cpl_hbm.at[i, pl.ds(start, n)], cpl_ref.at[i], sem.at[i])
            fetch.start()
            fetches.append(fetch)
        if first:
            for i in range(leaves):
                solved = dot(rhs_ref[i].astype(BF16), inv_ref[i], 0, 1)
                fwd_ref[i] = solved
                rnd_ref[i] = solved.astype(BF16)
        get_pattern.wait()
        sums = [None] * n
        for i in range(leaves):
            fetches[i].wait()
            for k in range(n):
                present = (pat_ref[start + k, i] != 0).astype(BF16)
                term = dot(rnd_ref[i] * present, cpl_ref[i, k], 1, 1)
                sums[k] = term if sums[k] is None else sums[k] + term
        own_rhs = top_ref[0].T
        for k in range(n):
            mine = (level_of_own_node() == start + k).astype(F32)
            split_columns(sums[k] - mine * own_rhs, keep_ref, send_ref, k)

    outs = [((n, half, width), F32)] * 2 + [((leaves, n, width, width), BF16)]
    ins = [top_rhs]
    if first:
        outs += [((leaves, columns, width), F32), ((leaves, columns, width), BF16)]
        ins += [right_hand, inverse]
    else:
        ins += [rounded]
    return call(
        kernel,
        "leaf_first" if first else "leaf_rest",
        outs,
        ins,
        2 * leaves * (n + first) * columns * width * width,
        hbm_ins=[pattern, coupling],
        scratch=[
            pltpu.SMEM(pattern.shape, jnp.int32),
            pltpu.SemaphoreType.DMA,
            pltpu.SemaphoreType.DMA((leaves,)),
        ],
    )


def own_factors(top_inverse, top_coupling):
    _, depth, width, _ = top_coupling.shape

    def kernel(inv_hbm, cpl_hbm, out_ref, raw, sem):
        a = pltpu.make_async_copy(inv_hbm.at[0], raw.at[0], sem.at[0])
        b = pltpu.make_async_copy(cpl_hbm.at[0, pl.ds(0, depth - 1)], raw.at[pl.ds(1, depth - 1)], sem.at[1])
        a.start()
        b.start()
        a.wait()
        b.wait()
        for k in range(depth):
            out_ref[k] = raw[k].astype(F32)

    return call(
        kernel,
        "own_factors",
        [((depth, width, width), F32)],
        [],
        hbm_ins=[top_inverse, top_coupling],
        scratch=[pltpu.VMEM((depth, width, width), BF16), pltpu.SemaphoreType.DMA((2,))],
    )[0]


def chip_factors(own, other):
    depth, width, _ = own.shape
    rows = width // 2

    def kernel(own_ref, other_ref, low_ref, high_ref, send_ref):
        def place(low, high, offset):
            for k in range(depth):
                low_ref[k] = low[k].astype(BF16)
            for k in range(depth - 1):
                high_ref[k] = high[k].astype(BF16)
            for k in range(depth - 2):
                send_ref[k] = high[k, offset : offset + rows]

        @pl.when(bit_of(0) == 0)
        def _():
            place(own_ref, other_ref, 0)

        @pl.when(bit_of(0) != 0)
        def _():
            place(other_ref, own_ref, rows)

    return call(
        kernel,
        "chip_factors",
        [((depth, width, width), BF16), ((depth - 1, width, width), BF16), ((depth - 2, rows, width), F32)],
        [own, other],
    )


def join_rows(mine, other, name):
    count, rows, width = mine.shape

    def kernel(mine_ref, other_ref, out_ref):
        @pl.when(bit_of(0) == 0)
        def _():
            out_ref[:, :rows] = mine_ref[...].astype(BF16)
            out_ref[:, rows:] = other_ref[...].astype(BF16)

        @pl.when(bit_of(0) != 0)
        def _():
            out_ref[:, rows:] = mine_ref[...].astype(BF16)
            out_ref[:, :rows] = other_ref[...].astype(BF16)

    return call(kernel, name, [((count, 2 * rows, width), BF16)], [mine, other])[0]


def pick(parts, b, count, name):
    _, rows, width = parts[0].shape

    def kernel(*refs):
        index = bit_of(b) << (b - 3)
        for i in range(3, b):
            index = index | (1 - bit_of(i)) << (i - 3)
        for m in range(1 << (b - 2)):

            @pl.when(index == m)
            def _(m=m):
                refs[-1][...] = refs[m][:count]

    return call(kernel, name, [((count, rows, width), F32)], parts[: 1 << (b - 2)])[0]


def node_up(mine, theirs, factors, level):
    half, width = mine.shape[-2:]

    def kernel(mine_ref, theirs_ref, w_ref, fwd_ref, up_ref):
        total = mine_ref[0] + theirs_ref[0]
        solved = dot((-total).astype(BF16), w_ref[0], 1, 1)
        fwd_ref[...] = solved
        rounded = solved.astype(BF16)
        for k in range(level):
            up_ref[k] = dot(rounded, w_ref[1 + k], 1, 1)

    return call(
        kernel,
        f"node_up_{level}",
        [((half, width), F32), ((level, half, width), F32)],
        [mine, theirs, factors],
        2 * (1 + level) * half * width * width,
    )


def add_terms(up, mine, theirs):
    level, half, width = up.shape

    def kernel(up_ref, mine_ref, theirs_ref, next_ref, *rest_ref):
        for k in range(level):
            total = up_ref[k] + (mine_ref[k] + theirs_ref[k])
            if k == level - 1:
                next_ref[0] = total
            else:
                rest_ref[0][k] = total

    outs = [((1, half, width), F32)]
    if level > 1:
        outs.append(((level - 1, half, width), F32))
    return call(kernel, f"add_terms_{level}", outs, [up, mine, theirs])


def top_down(mine, theirs, forwards, factors):
    half, width = mine.shape[-2:]
    levels = len(factors)
    n = len(forwards)

    def kernel(mine_ref, theirs_ref, *refs):
        fwd, w, out = refs[:n], refs[n : n + levels], refs[n + levels]
        total = mine_ref[0] + theirs_ref[0]
        base = dot((-total).astype(BF16), w[0][0], 1, 1)
        rounded = []
        for level in range(levels):
            if level > 0:
                carried = dot(rounded[0], w[level][1], 1, 0)
                for k in range(1, level):
                    carried = carried + dot(rounded[k], w[level][1 + k], 1, 0)
                base = fwd[level - 1][...] - carried
            solved = dot(base.astype(BF16), w[level][0], 1, 0)
            out[level] = solved
            rounded.append(solved.astype(BF16))

    return call(
        kernel,
        "top_down",
        [((levels, half, width), F32)],
        [mine, theirs, *forwards, *factors],
        2 * (levels + 1) * half * width * width,
    )[0]


def node_down(b, mine, theirs, forward, factors):
    level, half, width = mine.shape

    def kernel(mine_ref, theirs_ref, fwd_ref, w_ref, out_ref):
        take = bit_of(b) != 0
        carried = None
        for k in range(level):
            known = jnp.where(take, theirs_ref[k], mine_ref[k])
            out_ref[k] = known
            term = dot(known.astype(BF16), w_ref[1 + k], 1, 0)
            carried = term if carried is None else carried + term
        base = (fwd_ref[...] - carried).astype(BF16)
        out_ref[level] = dot(base, w_ref[0], 1, 0)

    return call(
        kernel,
        f"node_down_{level}",
        [((level + 1, half, width), F32)],
        [mine, theirs, forward, factors],
        2 * (1 + level) * half * width * width,
    )[0]


def leaf_down(pattern, mine, theirs, forward, inverse, couplings):
    leaves, columns, width = forward.shape
    depth, half, _ = mine.shape
    n = len(couplings)
    where = [(g, k) for g in range(n) for k in range(couplings[g].shape[1])]

    def kernel(pat_hbm, *refs):
        mine_ref, theirs_ref, fwd_ref, inv_ref = refs[:4]
        cpl = refs[4 : 4 + n]
        out_hbm, top_hbm, out, top, path, pat_ref, pat_sem, sem = refs[4 + n :]
        get_pattern = pltpu.make_async_copy(pat_hbm, pat_ref, pat_sem)
        get_pattern.start()
        own = jnp.maximum(level_of_own_node(), 0)

        def gather(low, high):
            for k in range(depth):
                path[k, :half] = low[k].astype(BF16)
                path[k, half:] = high[k].astype(BF16)
            top[...] = jnp.concatenate([low[own], high[own]], axis=0).T

        @pl.when(bit_of(0) == 0)
        def _():
            gather(mine_ref, theirs_ref)

        @pl.when(bit_of(0) != 0)
        def _():
            gather(theirs_ref, mine_ref)

        put_top = pltpu.make_async_copy(top, top_hbm.at[0], sem.at[leaves])
        put_top.start()
        get_pattern.wait()
        puts = []
        for i in range(leaves):
            carried = None
            for level, (g, k) in enumerate(where):
                present = (pat_ref[level, i] != 0).astype(BF16)
                term = dot(path[level] * present, cpl[g][i, k], 1, 0)
                carried = term if carried is None else carried + term
            base = (fwd_ref[i] - carried).astype(BF16)
            out[i] = dot(base, inv_ref[i], 1, 0).T
            put = pltpu.make_async_copy(out.at[i], out_hbm.at[i], sem.at[i])
            put.start()
            puts.append(put)
        for put in puts:
            put.wait()
        put_top.wait()

    return call(
        kernel,
        "leaf_down",
        [],
        [mine, theirs, forward, inverse, *couplings],
        2 * leaves * (depth + 1) * columns * width * width,
        hbm_ins=[pattern],
        hbm_outs=[((leaves, width, columns), F32), ((1, width, columns), F32)],
        scratch=[
            pltpu.VMEM((leaves, width, columns), F32),
            pltpu.VMEM((width, columns), F32),
            pltpu.VMEM((depth, columns, width), BF16),
            pltpu.SMEM(pattern.shape, jnp.int32),
            pltpu.SemaphoreType.DMA,
            pltpu.SemaphoreType.DMA((leaves + 1,)),
        ],
    )


def local(
    leaf_right_hand,
    leaf_diagonal_inverse,
    leaf_coupling,
    leaf_pattern,
    top_rhs,
    top_inverse,
    top_coupling,
):
    depth = lax.axis_size("col").bit_length() - 1
    pattern = leaf_pattern.T

    own = own_factors(top_inverse, top_coupling)
    low, high, to_hub = chip_factors(own, swap(own, 1))
    factors = [None] * depth
    factors[depth - 1] = low
    factors[depth - 2] = high

    keep, send, cpl_last, forward, rounded = leaf_terms(
        True,
        pattern,
        leaf_coupling,
        (depth - 1,),
        top_rhs,
        leaf_right_hand,
        leaf_diagonal_inverse,
    )
    keep_rest, send_rest, cpl_rest = leaf_terms(
        False, pattern, leaf_coupling, tuple(range(depth - 1)), top_rhs, rounded=rounded
    )

    hub = swap(to_hub, 2)
    factors[depth - 3] = join_rows(hub, swap(hub, 1), "join_hub")
    spread = [swap(hub[: depth - 3], 4 | m << 3) for m in range(1 << (depth - 3))]
    for b in range(3, depth):
        level = depth - 1 - b
        part = pick(spread, b, level + 1, f"pick_{level}")
        factors[level] = join_rows(part, swap(part, 1), f"join_{level}")

    mine, theirs = keep, swap(send, 1)
    rest, their_rest = keep_rest, swap(send_rest, 1)
    forwards = [None] * depth
    for level in reversed(range(1, depth)):
        forwards[level], up = node_up(mine, theirs, factors[level], level)
        mine, *rest = add_terms(up, rest, their_rest)
        mask = 1 << (depth - level)
        theirs = swap(mine, mask)
        if rest:
            rest = rest[0]
            their_rest = swap(rest, mask)

    known = top_down(mine, theirs, forwards[1 : depth - 2], factors[: depth - 2])
    for level in (depth - 2, depth - 1):
        b = depth - level
        known = node_down(b, known, swap(known, 1 << b), forwards[level], factors[level])
    return leaf_down(
        pattern, known, swap(known, 1), forward, leaf_diagonal_inverse, [cpl_rest, cpl_last]
    )


def solution(mesh):
    in_specs = (
        P(("grp", "col"), None, None),
        P(("grp", "col"), None, None),
        P(("grp", "col"), None, None, None),
        P(("grp", "col"), None),
        P(("grp", "col"), None, None),
        P(("grp", "col"), None, None),
        P(("grp", "col"), None, None, None),
    )
    out_specs = (P(("grp", "col"), None, None), P(("grp", "col"), None, None))
    return jax.shard_map(local, mesh=mesh, in_specs=in_specs, out_specs=out_specs, check_vma=False)
```
